256 devices in a mesh: cfg: 2 (over x_hi), seq: 64 (over x_lo, z, y), clip: 2 (over core).
Axes of the slice: x: 4 (x_hi: 2, x_lo: 2; x = x_hi * 2 + x_lo), y: 4, z: 8, core: 2. Of those that a mesh axis runs over, the one named last changes fastest.
Arguments:
- clean: bfloat16 [128, 256, 1152], P(('clip', 'seq')), parts along dimension 0, may hold values from -6 to 6
- noise: bfloat16 [128, 256, 1152], P(('clip', 'seq')), parts along dimension 0, may hold values from -6 to 6
- timestep: float32 [2], P('clip'), parts along dimension 0, may hold values from 0.1 to 0.9
- guidance: float32 [2], P('clip'), parts along dimension 0, may hold values from 2 to 6
- condition_vector: bfloat16 [2304], P('clip'), parts along dimension 0, may hold values from -6 to 6
- empty_prompt_vector: bfloat16 [1152], replicated, may hold values from -6 to 6
- timestep_direction: bfloat16 [1152], replicated, may hold values from -6 to 6
- spatial_query_key_value: bfloat16 [3, 1152, 1152], P(None, None, ('cfg', 'seq')), may hold values from -1 to 1
- spatial_output_weight: bfloat16 [1152, 1152], P(('cfg', 'seq')), may hold values from -0.1875 to 0.1875
- temporal_query_key_value: bfloat16 [3, 1152, 1152], P(None, None, ('cfg', 'seq')), may hold values from -1 to 1
- temporal_output_weight: bfloat16 [1152, 1152], P(('cfg', 'seq')), may hold values from -0.1875 to 0.1875
- adapter_down_maps: bfloat16 [2, 1152, 64], replicated, may hold values from -0.1875 to 0.1875
- adapter_up_maps: bfloat16 [2, 64, 1152], replicated, may hold values from -0.75 to 0.75
Outputs:
- student_out: bfloat16 [128, 256, 1152], P(('clip', 'seq'), 'cfg'), parts along dimension 0
- student_tangent: bfloat16 [128, 256, 1152], P(('clip', 'seq'), 'cfg'), parts along dimension 0
The draws below stay inside these ranges and needn't reach their ends.
There are 2 independent parts, one for each index of `clip`. The reference program is written for one: setup_inputs(seed, part) draws one part's arguments, and reference() takes and returns one part's arrays. A program takes and returns all parts, laid end to end along the dimension named above; an argument that names none is the same for every part. Nothing has to cross between parts.
All inputs are finite; a program needn't handle non-finite values.
Results may differ from the reference program's by a relative error of at most 0.028.
Values may be sent and summed in bfloat16 or wider, within the bound.
A program may use at most 128 MiB of HBM per device.

```python
import math
import jax
import jax.numpy as jnp
from jax import lax

MODEL_WIDTH = 1152
HEAD_DIM = 72
FRAMES = 64
POSITIONS = 256
ADAPTER_RANK = 64


def projection_draw(seed_key, salt):
    folded = jax.random.fold_in(seed_key, salt)
    first_key = jax.random.fold_in(folded, 0)
    gaussian = jax.random.normal(first_key, (3, MODEL_WIDTH, MODEL_WIDTH), jnp.float32) / math.sqrt(MODEL_WIDTH)
    return jnp.clip(gaussian, -1.0, 1.0).astype(jnp.bfloat16)


def draw_spatial_query_key_value(key, part):
    return projection_draw(key, 101)


def draw_temporal_query_key_value(key, part):
    return projection_draw(key, 202)


def shard_levels(key, dims, shards, smallest, largest):
    def one(dim, blocks):
        heights = jax.random.uniform(jax.random.fold_in(jax.random.fold_in(key, 6), dim), (blocks,), jnp.float32, smallest / len(shards), largest / len(shards))
        return jnp.repeat(jnp.exp(heights), dims[dim] // blocks).reshape((-1,) + (1,) * (len(dims) - dim - 1))

    level = one(*shards[0])
    for cut in shards[1:]:
        level = level * one(*cut)
    return level


def bell_draw(key, extent, width, bound, cuts=(), dtype=jnp.bfloat16):
    gain = shard_levels(key, extent, cuts, -0.22, 0.18) if cuts else 1.0
    values = jax.random.normal(key, extent, jnp.float32) * width * gain
    return jnp.minimum(jnp.maximum(values, -bound), bound).astype(dtype)


def setup_inputs(seed: int = 0, part: int = 0) -> dict:
    splits = jax.random.split(jax.random.key(seed), 14)
    own_keys = jax.random.split(jax.random.fold_in(splits[13], part), 14)
    clean = bell_draw(own_keys[0], (FRAMES, POSITIONS, MODEL_WIDTH), 1.0, 6.0, ((0, 64),))
    noise = bell_draw(own_keys[1], (FRAMES, POSITIONS, MODEL_WIDTH), 1.0, 6.0, ((0, 64),))
    timestep = jnp.clip(jax.random.uniform(own_keys[2], (1,), jnp.float32, 0.1, 0.9), 0.1, 0.9)
    guidance = jnp.clip(jax.random.uniform(own_keys[3], (1,), jnp.float32, 2.0, 6.0), 2.0, 6.0)
    condition_vector = bell_draw(own_keys[4], (MODEL_WIDTH,), 1.0, 6.0)
    empty_prompt_vector = bell_draw(splits[5], (MODEL_WIDTH,), 1.0, 6.0)
    timestep_direction = bell_draw(splits[6], (MODEL_WIDTH,), 1.0, 6.0)
    spatial_query_key_value = draw_spatial_query_key_value(jax.random.fold_in(splits[13], 71), part)
    spatial_output_weight = bell_draw(splits[8], (MODEL_WIDTH, MODEL_WIDTH), MODEL_WIDTH ** -0.5, 0.1875, ((0, 128),))
    temporal_query_key_value = draw_temporal_query_key_value(jax.random.fold_in(splits[13], 71), part)
    temporal_output_weight = bell_draw(splits[10], (MODEL_WIDTH, MODEL_WIDTH), MODEL_WIDTH ** -0.5, 0.1875, ((0, 128),))
    adapter_down_maps = bell_draw(splits[11], (2, MODEL_WIDTH, ADAPTER_RANK), MODEL_WIDTH ** -0.5, 0.1875)
    adapter_up_maps = bell_draw(splits[12], (2, ADAPTER_RANK, MODEL_WIDTH), ADAPTER_RANK ** -0.5, 0.75)
    return {"clean": clean, "noise": noise, "timestep": timestep, "guidance": guidance, "condition_vector": condition_vector, "empty_prompt_vector": empty_prompt_vector, "timestep_direction": timestep_direction, "spatial_query_key_value": spatial_query_key_value, "spatial_output_weight": spatial_output_weight, "temporal_query_key_value": temporal_query_key_value, "temporal_output_weight": temporal_output_weight, "adapter_down_maps": adapter_down_maps, "adapter_up_maps": adapter_up_maps}


epsilon = 1e-06

def rms_scale(features):
    return features * lax.rsqrt(lax.optimization_barrier(jnp.mean(features * features, axis=-1, keepdims=True)) + epsilon)

def project(rows_in, matrix):
    return jnp.einsum('...d,dk->...k', rows_in.astype(jnp.float32), matrix.astype(jnp.float32))

def space_attend(queries, key_rows, value_rows):
    head_count = queries.shape[-1] // HEAD_DIM
    split_dims = queries.shape[:-1] + (head_count, HEAD_DIM)
    scores = jnp.einsum('...qhd,...khd->...hqk', queries.reshape(split_dims).astype(jnp.float32), key_rows.reshape(split_dims).astype(jnp.float32)) * HEAD_DIM ** (-0.5)
    scores = scores - lax.optimization_barrier(jnp.max(scores, axis=-1, keepdims=True))
    exponent = jnp.exp(scores)
    soft_weights = (exponent / lax.optimization_barrier(jnp.sum(exponent, axis=-1, keepdims=True))).astype(jnp.bfloat16)
    result = jnp.einsum('...hqk,...khd->...qhd', soft_weights.astype(jnp.float32), value_rows.reshape(split_dims).astype(jnp.float32))
    return result.astype(jnp.bfloat16).reshape(queries.shape)

def time_attend(queries, key_rows, value_rows):
    head_count = queries.shape[-1] // HEAD_DIM
    split_dims = queries.shape[:-1] + (head_count, HEAD_DIM)
    scores = jnp.einsum('...fxhd,...gxhd->...xhfg', queries.reshape(split_dims).astype(jnp.float32), key_rows.reshape(split_dims).astype(jnp.float32)) * HEAD_DIM ** (-0.5)
    scores = scores - lax.optimization_barrier(jnp.max(scores, axis=-1, keepdims=True))
    exponent = jnp.exp(scores)
    soft_weights = (exponent / lax.optimization_barrier(jnp.sum(exponent, axis=-1, keepdims=True))).astype(jnp.bfloat16)
    result = jnp.einsum('...xhfg,...gxhd->...fxhd', soft_weights.astype(jnp.float32), value_rows.reshape(split_dims).astype(jnp.float32))
    return result.astype(jnp.bfloat16).reshape(queries.shape)

def time_core(embedding_rows, query_weight, key_weight, value_weight, out_weight):
    normed = rms_scale(embedding_rows).astype(jnp.bfloat16)
    queries = project(normed, query_weight).astype(jnp.bfloat16)
    key_rows = project(normed, key_weight).astype(jnp.bfloat16)
    value_rows = project(normed, value_weight).astype(jnp.bfloat16)
    return project(time_attend(queries, key_rows, value_rows), out_weight)

def student_network(embedding_rows, query_weight, key_weight, value_weight, out_weight, down_query, query_up_map, down_value, value_up_map):
    normed = rms_scale(embedding_rows).astype(jnp.bfloat16)
    low_query = project(normed, down_query).astype(jnp.bfloat16)
    low_value = project(normed, down_value).astype(jnp.bfloat16)
    queries = (project(normed, query_weight) + project(low_query, query_up_map)).astype(jnp.bfloat16)
    key_rows = project(normed, key_weight).astype(jnp.bfloat16)
    value_rows = (project(normed, value_weight) + project(low_value, value_up_map)).astype(jnp.bfloat16)
    return project(time_attend(queries, key_rows, value_rows), out_weight)

def reference(clean, noise, timestep, guidance, condition_vector, empty_prompt_vector, timestep_direction, spatial_query_key_value, spatial_output_weight, temporal_query_key_value, temporal_output_weight, adapter_down_maps, adapter_up_maps):
    moment = timestep[0]
    strength = guidance[0]
    noisy_rows = ((1.0 - moment) * clean.astype(jnp.float32) + moment * noise.astype(jnp.float32)).astype(jnp.bfloat16)
    shifted = noisy_rows.astype(jnp.float32) + moment * timestep_direction.astype(jnp.float32)
    velocities = []
    for embedding_rows in (condition_vector, empty_prompt_vector):
        entries = shifted + embedding_rows.astype(jnp.float32)
        normed = rms_scale(entries).astype(jnp.bfloat16)
        queries = project(normed, spatial_query_key_value[0]).astype(jnp.bfloat16)
        key_rows = project(normed, spatial_query_key_value[1]).astype(jnp.bfloat16)
        value_rows = project(normed, spatial_query_key_value[2]).astype(jnp.bfloat16)
        attended = lax.map(lambda trio: space_attend(trio[0], trio[1], trio[2]), (queries, key_rows, value_rows))
        layer_one = (entries + project(attended, spatial_output_weight)).astype(jnp.bfloat16)
        partial_value = time_core(layer_one.astype(jnp.float32), temporal_query_key_value[0], temporal_query_key_value[1], temporal_query_key_value[2], temporal_output_weight)
        velocities.append((layer_one.astype(jnp.float32) + partial_value).astype(jnp.bfloat16))
    cond_velocity = velocities[0].astype(jnp.float32)
    uncond_velocity = velocities[1].astype(jnp.float32)
    guided = (uncond_velocity + strength * (cond_velocity - uncond_velocity)).astype(jnp.bfloat16)
    student_in = shifted + condition_vector.astype(jnp.float32)

    def student_map(embedding_rows):
        return student_network(embedding_rows, temporal_query_key_value[0], temporal_query_key_value[1], temporal_query_key_value[2], temporal_output_weight, adapter_down_maps[0], adapter_up_maps[0], adapter_down_maps[1], adapter_up_maps[1])
    partial_value, tangent_part = jax.jvp(student_map, (student_in,), (guided.astype(jnp.float32),))
    student_out = (student_in + partial_value).astype(jnp.bfloat16)
    student_tangent = (guided.astype(jnp.float32) + tangent_part).astype(jnp.bfloat16)
    return (student_out, student_tangent)
```

```python
import functools

import jax
import jax.numpy as jnp
from jax import lax
from jax.experimental import pallas as pl
from jax.experimental.pallas import tpu as pltpu
from jax.sharding import PartitionSpec as P

MESH = pl.DeviceIdType.MESH
HEAD_DIM = 72
PIECE = 9
SCALE = HEAD_DIM ** (-0.5)
epsilon = 1e-06
F32 = jnp.float32
BF16 = jnp.bfloat16

NX, NY, NZ = 4, 4, 8
QKV_ROWS = 32
CHUNK_ROWS = 48


def dot_nt(a, b):
    return lax.dot_general(a, b, (((1,), (1,)), ((), ())), preferred_element_type=F32)


def dot_nn(a, b):
    return lax.dot_general(a, b, (((1,), (0,)), ((), ())), preferred_element_type=F32)


class Copies:
    def __init__(self, send_sem, recv_sem, names):
        self.send_sem, self.recv_sem = send_sem, recv_sem
        self.ids = {name: i for i, name in enumerate(names)}
        self.sent = []

    def _id(self, name):
        return self.ids[name]

    def send(self, name, src, dst, target):
        i = self._id(name)
        copy = pltpu.make_async_remote_copy(
            src_ref=src, dst_ref=dst, send_sem=self.send_sem.at[i], recv_sem=self.recv_sem.at[i],
            device_id=target, device_id_type=MESH,
        )
        copy.start()
        self.sent.append(copy)

    def recv(self, name, dst, target):
        i = self._id(name)
        pltpu.make_async_remote_copy(
            src_ref=dst, dst_ref=dst, send_sem=self.send_sem.at[i], recv_sem=self.recv_sem.at[i],
            device_id=target, device_id_type=MESH,
        ).wait_recv()

    def finish(self):
        for copy in self.sent:
            copy.wait_send()


ALL = slice(None)
LOW, HIGH = pl.ds(0, 2), pl.ds(2, 2)


def copy_names(layer):
    names = [("minor", layer, d) for d in (1, 2, 3)]
    names += [(way, layer, k) for way in ("up", "down") for k in range(4)]
    names += [(way, layer, j) for way in ("right", "left", "fright", "fleft") for j in range(8)]
    return names + [("sib", c, layer, q, j) for c in range(2) for q in range(4) for j in range(8)]


def gather_kernel(layers, chunk_ref, w_ref, send_sem, recv_sem, local_sem):
    cfg, seq, core = lax.axis_index("cfg"), lax.axis_index("seq"), lax.axis_index("clip")
    x = cfg * 2 + seq // 32
    z = (seq % 32) // 4
    y = seq % 4

    def run(color):
        rows = pl.ds(24 * color, 24)
        minor, major = (y, x) if color == 0 else (x, y)

        def device(mj, zz, mn, which=color):
            xx, yy = (mj, mn) if color == 0 else (mn, mj)
            return (xx // 2, (xx % 2) * 32 + zz * 4 + yy, which)

        def block(layer, mj, zz, mn=ALL, own=color):
            xx, yy = (mj, mn) if own == 0 else (mn, mj)
            return w_ref.at[layer, xx, zz, yy, pl.ds(24 * own, 24)]

        def mod4(a):
            return (a + 4) % 4

        def mod8(a):
            return (a + 8) % 8

        sibling = device(major, z, minor, 1 - color)
        up, down = device(major, mod8(z + 1), minor), device(major, mod8(z - 1), minor)
        right, left = device(mod4(major + 1), z, minor), device(mod4(major - 1), z, minor)
        ring = [device(major, z, mod4(minor + d)) for d in (1, 2, 3)]

        barrier = pltpu.get_barrier_semaphore()
        peers = ring + [up, down, right, left, sibling]
        for peer in peers:
            pl.semaphore_signal(barrier, inc=1, device_id=peer, device_id_type=MESH)
        pl.semaphore_wait(barrier, len(peers))

        copies = Copies(send_sem, recv_sem, [n for layer in range(layers) for n in copy_names(layer)])

        for layer in range(layers):
            own = chunk_ref.at[layer, rows]
            here = block(layer, major, z, minor)
            for d in (1, 2, 3):
                copies.send(("minor", layer, d), own, here, ring[d - 1])
            keep = pltpu.make_async_copy(own, here, local_sem.at[layer])
            keep.start()

        def arrived_minor(layer):
            own = chunk_ref.at[layer, rows]
            here = block(layer, major, z, minor)
            pltpu.make_async_copy(own, here, local_sem.at[layer]).wait()
            for d in (1, 2, 3):
                copies.recv(("minor", layer, d), block(layer, major, z, mod4(minor - d)), sibling)

        def spread(layer, j):
            b = block(layer, major, mod8(z + j))
            copies.send(("right", layer, j % 8), b, b, right)
            copies.send(("left", layer, j % 8), b, b, left)
            copies.send(("sib", color, layer, 0, j % 8), b, b, sibling)

        def z_send(layer, k):
            mn_up, mn_down = (ALL, ALL) if k < 3 else (LOW, HIGH)
            b = block(layer, major, mod8(z - k), mn_up)
            copies.send(("up", layer, k), b, b, up)
            b = block(layer, major, mod8(z + k), mn_down)
            copies.send(("down", layer, k), b, b, down)

        def z_recv(layer, k):
            mn_up, mn_down = (ALL, ALL) if k < 3 else (LOW, HIGH)
            copies.recv(("up", layer, k), block(layer, major, mod8(z - 1 - k), mn_up), sibling)
            copies.recv(("down", layer, k), block(layer, major, mod8(z + 1 + k), mn_down), sibling)

        groups = [(0,), (-1, 1), (-2, 2), (-3, 3), (4,)]

        def pass_on(layer, j):
            zz = mod8(z + j)
            copies.recv(("right", layer, j % 8), block(layer, mod4(major - 1), zz), sibling)
            b = block(layer, mod4(major - 1), zz)
            h = block(layer, mod4(major - 1), zz, LOW)
            copies.send(("fright", layer, j % 8), h, h, right)
            copies.send(("sib", color, layer, 1, j % 8), b, b, sibling)
            copies.recv(("left", layer, j % 8), block(layer, mod4(major + 1), zz), sibling)
            b = block(layer, mod4(major + 1), zz)
            h = block(layer, mod4(major + 1), zz, HIGH)
            copies.send(("fleft", layer, j % 8), h, h, left)
            copies.send(("sib", color, layer, 2, j % 8), b, b, sibling)

        def last(layer, j):
            zz = mod8(z + j)
            far = mod4(major + 2)
            copies.recv(("fright", layer, j % 8), block(layer, far, zz, LOW), sibling)
            copies.recv(("fleft", layer, j % 8), block(layer, far, zz, HIGH), sibling)
            b = block(layer, far, zz)
            copies.send(("sib", color, layer, 3, j % 8), b, b, sibling)

        for layer in range(layers):
            arrived_minor(layer)
            for k in range(5):
                if k > 0:
                    z_recv(layer, k - 1)
                if k < 4:
                    z_send(layer, k)
                for j in groups[k]:
                    spread(layer, j)
                if layer > 0:
                    for j in groups[k]:
                        pass_on(layer - 1, j)
        for k in range(5):
            for j in groups[k]:
                pass_on(layers - 1, j)
        for layer in range(layers):
            for k in range(5):
                for j in groups[k]:
                    last(layer, j)

        other = 1 - color
        other_major = y if color == 0 else x
        for layer in range(layers):
            for q, dm in enumerate((0, 3, 1, 2)):
                for k in range(5):
                    for j in groups[k]:
                        copies.recv(
                            ("sib", other, layer, q, j % 8),
                            block(layer, mod4(other_major + dm), mod8(z + j), ALL, other),
                            sibling,
                        )
        copies.finish()

    @pl.when(core == 0)
    def _():
        run(0)

    @pl.when(core == 1)
    def _():
        run(1)


def gather_weights(chunks):
    layers = chunks.shape[0]
    n = layers * len(copy_names(0))
    return pl.pallas_call(
        functools.partial(gather_kernel, layers),
        out_shape=jax.ShapeDtypeStruct((layers, NX, NZ, NY, CHUNK_ROWS, chunks.shape[-1]), BF16),
        in_specs=[pl.BlockSpec(memory_space=pl.ANY)],
        out_specs=pl.BlockSpec(memory_space=pl.ANY),
        scratch_shapes=[
            pltpu.SemaphoreType.DMA((n,)),
            pltpu.SemaphoreType.DMA((n,)),
            pltpu.SemaphoreType.DMA((layers,)),
        ],
        compiler_params=pltpu.CompilerParams(collective_id=0, has_side_effects=True),
        name="weights",
    )(chunks)


def wire_chunk(qkv, out):
    width = out.shape[-1]
    rows = jnp.transpose(qkv, (0, 2, 1)).reshape(3 * PIECE, width)
    zeros = lambda n: jnp.zeros((n, width), BF16)
    return jnp.concatenate([rows, zeros(QKV_ROWS - 3 * PIECE + 2), out, zeros(5)], axis=0)


def lanes(rows):
    return lax.broadcasted_iota(jnp.int32, (rows, 256), 1) % 32


def soft(scores):
    scores = scores - jnp.max(scores, axis=-1, keepdims=True)
    exponent = jnp.exp(scores)
    return exponent / jnp.sum(exponent, axis=-1, keepdims=True)


def head_parts(t):
    q = jnp.where(lanes(t.shape[0]) < PIECE, t, 0.0).astype(BF16)
    k = pltpu.roll(t, 256 - PIECE, 1).astype(BF16)
    return q, k, t.astype(BF16)


def pair_columns(first, second):
    shifted = pltpu.roll(second, 256 - 16, 1)
    return jnp.where(lanes(first.shape[0]) >= 16, first, shifted).astype(BF16)


def pair_weights(w_ref):
    width = w_ref.shape[-1]
    w = w_ref.reshape(16, CHUNK_ROWS, width)
    qkv = [w[8 * i : 8 * i + 8, :QKV_ROWS].reshape(256, width) for i in range(2)]
    out = [w[8 * i : 8 * i + 8, QKV_ROWS:].reshape(8, 1, 16, width) for i in range(2)]
    return qkv, jnp.concatenate([out[1], out[0]], axis=1).reshape(256, width)


def rms(e):
    return e * lax.rsqrt(jnp.mean(e * e, axis=-1, keepdims=True) + epsilon)


def space_kernel(moment_ref, clean_ref, noise_ref, dir_ref, emb_ref, w_ref, out_ref, entry, normed, acc):
    step = pl.program_id(0)

    @pl.when(step == 0)
    def _():
        t = moment_ref[0]
        noisy = ((1.0 - t) * clean_ref[...].astype(F32) + t * noise_ref[...].astype(F32)).astype(BF16)
        e = noisy.astype(F32) + t * dir_ref[...] + emb_ref[...]
        entry[...] = e
        normed[...] = rms(e).astype(BF16)
        acc[...] = jnp.zeros_like(acc)

    qkv, out_w = pair_weights(w_ref)
    mixed = []
    for i in range(2):
        t = dot_nt(normed[...], qkv[i])
        q, k, v = head_parts(t)
        weights = soft(dot_nt(q, k) * SCALE).astype(BF16)
        mixed.append(dot_nn(weights, v))
    acc[...] += dot_nn(pair_columns(*mixed), out_w)

    @pl.when(step == pl.num_programs(0) - 1)
    def _():
        out_ref[...] = (entry[...] + acc[...]).astype(BF16)


def w_spec(layer, width, steps=8):
    return pl.BlockSpec(
        (None, None, None, 16, CHUNK_ROWS, width),
        lambda i, *_: (layer, (i % 8) // 2, (i % 8) % 2, 0, 0, 0),
    )


def full(shape):
    return pl.BlockSpec(shape, lambda i: (0,) * len(shape))


def space_layer(moment, clean, noise, direction, emb, weights):
    rows, width = clean.shape
    return pl.pallas_call(
        space_kernel,
        grid=(8,),
        out_shape=jax.ShapeDtypeStruct((rows, width), BF16),
        in_specs=[
            pl.BlockSpec(memory_space=pltpu.SMEM),
            full((rows, width)),
            full((rows, width)),
            full((1, width)),
            full((1, width)),
            w_spec(0, width),
        ],
        out_specs=full((rows, width)),
        scratch_shapes=[
            pltpu.VMEM((rows, width), F32),
            pltpu.VMEM((rows, width), BF16),
            pltpu.VMEM((rows, width), F32),
        ],
        name="space",
    )(moment, clean, noise, direction, emb, weights)


def same_position(rows):
    a = lax.broadcasted_iota(jnp.int32, (rows, rows), 0)
    b = lax.broadcasted_iota(jnp.int32, (rows, rows), 1)
    return a % 2 == b % 2


NEG = -1e30


def time_kernel(
    scal_ref, teach_ref, noisy_ref, dir_ref, cond_ref, down_ref, up_ref, w_ref,
    out_ref, tan_ref, normed, student, entry, guide, acc,
):
    step = pl.program_id(0)
    half = noisy_ref.shape[0]
    width = noisy_ref.shape[1]

    @pl.when(step == 0)
    def _():
        normed[...] = rms(teach_ref[...].astype(F32)).astype(BF16)
        acc[...] = jnp.zeros_like(acc)

    @pl.when(step == 8)
    def _():
        velocity = (teach_ref[...].astype(F32) + acc[...]).astype(BF16).astype(F32)
        cond, uncond = velocity[:half], velocity[half:]
        guided = (uncond + scal_ref[1] * (cond - uncond)).astype(BF16).astype(F32)
        guide[...] = guided
        e = noisy_ref[...].astype(F32) + scal_ref[0] * dir_ref[...] + cond_ref[...]
        entry[...] = e
        scale = lax.rsqrt(jnp.mean(e * e, axis=-1, keepdims=True) + epsilon)
        cross = jnp.mean(e * guided, axis=-1, keepdims=True)
        student[:half, :width] = (e * scale).astype(BF16)
        student[half:, :width] = (scale * (guided - e * (scale * scale * cross))).astype(BF16)
        student[:, width:] = dot_nn(student[:, :width], down_ref[...]).astype(BF16)
        acc[...] = jnp.zeros_like(acc)

    qkv, out_w = pair_weights(w_ref)

    @pl.when(step < 8)
    def _():
        mixed = []
        same = same_position(half)
        for i in range(2):
            q, k, v = head_parts(dot_nt(normed[...], qkv[i]))
            parts = []
            for b in range(2):
                r = slice(b * half, (b + 1) * half)
                scores = jnp.where(same, dot_nt(q[r], k[r]) * SCALE, NEG)
                parts.append(dot_nn(soft(scores).astype(BF16), v[r]))
            mixed.append(jnp.concatenate(parts, axis=0))
        acc[...] += dot_nn(pair_columns(*mixed), out_w)

    @pl.when(step >= 8)
    def _():
        mixed = []
        same = same_position(half)
        for i in range(2):
            t = dot_nt(student[:, :width], qkv[i]) + dot_nt(student[:, width:], up_ref[i])
            q, k, v = head_parts(t)
            s = dot_nt(q, k) * SCALE
            weights = soft(jnp.where(same, s[:half, :half], NEG))
            ds = s[:half, half:] + s[half:, :half]
            dw = weights * (ds - jnp.sum(weights * ds, axis=-1, keepdims=True))
            weights, dw = weights.astype(BF16), dw.astype(BF16)
            top = jnp.concatenate([weights, jnp.zeros_like(weights)], axis=1)
            low = jnp.concatenate([dw, weights], axis=1)
            mixed.append(dot_nn(jnp.concatenate([top, low], axis=0), v))
        acc[...] += dot_nn(pair_columns(*mixed), out_w)

    @pl.when(step == pl.num_programs(0) - 1)
    def _():
        out_ref[...] = (entry[...] + acc[:half]).astype(BF16)
        tan_ref[...] = (guide[...] + acc[half:]).astype(BF16)


def time_layer(scalars, teach, noisy, direction, cond, down, up, weights):
    half, width = noisy.shape
    return pl.pallas_call(
        time_kernel,
        grid=(16,),
        out_shape=[jax.ShapeDtypeStruct((half, width), BF16)] * 2,
        in_specs=[
            pl.BlockSpec(memory_space=pltpu.SMEM),
            full((2 * half, width)),
            full((half, width)),
            full((1, width)),
            full((1, width)),
            full(down.shape),
            pl.BlockSpec((None, 2, 256, 128), lambda i: (jnp.maximum(i - 8, 0), 0, 0, 0)),
            w_spec(1, width),
        ],
        out_specs=[full((half, width))] * 2,
        scratch_shapes=[
            pltpu.VMEM((2 * half, width), BF16),
            pltpu.VMEM((2 * half, width + 128), BF16),
            pltpu.VMEM((half, width), F32),
            pltpu.VMEM((half, width), F32),
            pltpu.VMEM((2 * half, width), F32),
        ],
        name="time",
    )(scalars, teach, noisy, direction, cond, down, up, weights)


def tangled_up(up_maps):
    rank, width = up_maps.shape[1], up_maps.shape[2]
    rows = jnp.transpose(up_maps, (0, 2, 1)).reshape(2, width // PIECE, PIECE, rank)
    query = jnp.pad(rows[0], ((0, 0), (0, QKV_ROWS - PIECE), (0, 0)))
    value = jnp.pad(rows[1], ((0, 0), (2 * PIECE, QKV_ROWS - 3 * PIECE), (0, 0)))
    return jnp.concatenate([query, value], axis=-1).reshape(8, 2, 256, 2 * rank)


def on_device(
    clean, noise, timestep, guidance, condition_vector, empty_prompt_vector, timestep_direction,
    spatial_query_key_value, spatial_output_weight, temporal_query_key_value, temporal_output_weight,
    adapter_down_maps, adapter_up_maps,
):
    side = lax.axis_index("cfg")
    width = clean.shape[-1]
    positions = clean.shape[1]
    moment = timestep[0]
    chunks = jnp.stack(
        [
            wire_chunk(spatial_query_key_value, spatial_output_weight),
            wire_chunk(temporal_query_key_value, temporal_output_weight),
        ]
    )
    weights = gather_weights(chunks)
    weights = weights.reshape(2, NX, 2, 16, CHUNK_ROWS, width)
    direction = timestep_direction.astype(F32)[None]
    cond = condition_vector.astype(F32)[None]
    emb = jnp.where(side == 0, condition_vector, empty_prompt_vector).astype(F32)[None]
    layer_one = space_layer(timestep, clean[0], noise[0], direction, emb, weights)
    teach = lax.all_to_all(
        layer_one.reshape(positions // 2, 2, width), ("cfg", "seq"), split_axis=0, concat_axis=0, tiled=True
    ).reshape(positions, width)
    half = positions // 2
    own = lambda a: lax.dynamic_slice_in_dim(a[0], side * half, half, 0).astype(F32)
    noisy = ((1.0 - moment) * own(clean) + moment * own(noise)).astype(BF16)
    noisy = lax.all_to_all(
        noisy.reshape(half // 2, 2, width), "seq", split_axis=0, concat_axis=0, tiled=True
    ).reshape(half, width)
    down = jnp.transpose(adapter_down_maps, (1, 0, 2)).reshape(width, -1)
    scalars = jnp.concatenate([timestep, guidance])
    primal, tangent = time_layer(
        scalars, teach, noisy, direction, cond, down, tangled_up(adapter_up_maps), weights
    )
    returned = lax.all_to_all(
        jnp.stack([primal, tangent]).reshape(2, half // 2, 2, width), "seq", split_axis=1, concat_axis=1, tiled=True
    ).reshape(2, 1, half, width)
    return returned[0], returned[1]


def solution(mesh):
    return jax.shard_map(
        on_device,
        mesh=mesh,
        in_specs=(
            P(("clip", "seq"), None, None),
            P(("clip", "seq"), None, None),
            P("clip"),
            P("clip"),
            P("clip"),
            P(),
            P(),
            P(None, None, ("cfg", "seq")),
            P(("cfg", "seq"), None),
            P(None, None, ("cfg", "seq")),
            P(("cfg", "seq"), None),
            P(),
            P(),
        ),
        out_specs=(P(("clip", "seq"), "cfg", None), P(("clip", "seq"), "cfg", None)),
        check_vma=False,
    )
```
